32 devices in a mesh: seq: 32 (over z, y, x, core).
Axes of the slice: x: 2, y: 2, z: 4, core: 2. Of those that a mesh axis runs over, the one named last changes fastest.
Arguments:
- hidden: bfloat16 [4096, 2048], P('seq'), may hold values from -6 to 6
- queries: bfloat16 [4096, 2048], P('seq'), may hold values from -6 to 6
- key_rows: bfloat16 [4096, 512], P('seq'), may hold values from -6 to 6
- grad_out: bfloat16 [4096, 2048], P('seq'), may hold values from -6 to 6
- master_value: float32 [2048, 512], P('seq'), may hold values from -0.125 to 0.125
- adam_first: float32 [2048, 512], P('seq'), may hold values from -12 to 12
- adam_second: float32 [2048, 512], P('seq'), may hold values from 1 to 100
Outputs:
- attention: bfloat16 [4096, 2048], P('seq')
- grad_queries: bfloat16 [4096, 2048], P('seq')
- grad_keys: bfloat16 [4096, 512], P('seq')
- grad_hidden: bfloat16 [4096, 2048], P('seq')
- new_master: float32 [2048, 512], P('seq')
- new_first: float32 [2048, 512], P('seq')
- new_second: float32 [2048, 512], P('seq')
The draws below stay inside these ranges and needn't reach their ends.
All inputs are finite; a program needn't handle non-finite values.
Results may differ from the reference program's by a relative error of at most 0.02.
Values may be sent and summed in bfloat16 or wider, within the bound.
No kernel may reach another device: no remote copies, remote signals or barrier semaphores. Data moves between devices by JAX's collectives and lax.ppermute only.
A program may use at most 64 MiB of HBM per device.

```python
import math
import jax
import jax.numpy as jnp
from jax import lax

DW = 2048
HQ = 16
HK = 4
DH = 128
WINDOW = 512
OPT_STEP = 10
TOK_DEV = 128
SEQ = 4096
QW = 2048
KVW = 512


def draw_queries(key, part):
    entries = jnp.clip(jax.random.normal(jax.random.fold_in(key, 1), (SEQ, HQ * DH), jnp.float32), -6.0, 6.0)
    return entries.astype(jnp.bfloat16)


def draw_key_rows(key, part):
    entries = jnp.clip(jax.random.normal(jax.random.fold_in(key, 2), (SEQ, HK * DH), jnp.float32), -6.0, 6.0)
    return entries.astype(jnp.bfloat16)


def strengthened(array, key, source, target, shards_of, factor):
    owner, partner = [(jnp.arange(array.shape[dim]) // (array.shape[dim] // shards_of)).reshape([-1 if axis == dim else 1 for axis in range(array.ndim)]) for dim in (source, target)]
    chosen = jax.random.permutation(key, shards_of)[partner]
    strong = (owner == chosen) | (owner == (partner + shards_of // 2) % shards_of)
    return jnp.where(strong, factor * array, array)


def block_scale(stream_key, dims, cuts, smallest, largest):
    level, own = 1.0, jax.random.fold_in(stream_key, 6)
    for position, parts in cuts:
        steps = jnp.exp(jax.random.uniform(jax.random.fold_in(own, position), (parts,), jnp.float32, smallest / len(cuts), largest / len(cuts)))
        level = level * jnp.repeat(steps, dims[position] // parts).reshape([-1 if axis == position else 1 for axis in range(len(dims))])
    return level


def gaussian(stream_key, shape, deviation, bound, cuts=(), held_as=jnp.bfloat16):
    level = block_scale(stream_key, shape, cuts, -0.22, 0.18) if cuts else 1.0
    array = jax.random.normal(stream_key, shape, jnp.float32) * deviation * level
    return jnp.minimum(jnp.maximum(array, -bound), bound).astype(held_as)


def bell_draw_with(own_key, shape, scale, reach, shards, heavy, kind=jnp.bfloat16):
    array = scale * jax.random.normal(own_key, shape, jnp.float32)
    if shards:
        array = array * block_scale(own_key, shape, shards, -0.22, 0.18)
    return jnp.clip(strengthened(array, jax.random.fold_in(own_key, 3), *heavy), -reach, reach).astype(kind)


def setup_inputs(seed: int = 0) -> dict:
    arg_keys = jax.random.split(jax.random.key(seed), 8)
    hidden = bell_draw_with(arg_keys[0], (SEQ, DW), 1.0, 6.0, ((0, 32),), (0, 1, 32, 2.75))
    queries = draw_queries(jax.random.fold_in(arg_keys[7], 71), 0)
    key_rows = draw_key_rows(jax.random.fold_in(arg_keys[7], 71), 0)
    grad_out = gaussian(arg_keys[3], (SEQ, QW), 1.0, 6.0, ((0, 32),))
    master_value = gaussian(arg_keys[4], (DW, KVW), DW ** -0.5, 0.125, ((0, 32),), jnp.float32)
    adam_first = gaussian(arg_keys[5], (DW, KVW), 2.0, 12.0, ((0, 32),), jnp.float32)
    adam_second = jnp.clip(jnp.exp(math.log(100.0) - 4.6051702 * jax.random.uniform(arg_keys[6], (DW, KVW), jnp.float32) ** block_scale(arg_keys[6], (DW, KVW), ((0, 32),), -0.2, 0.2)), 1.0, 100.0)
    return {"hidden": hidden, "queries": queries, "key_rows": key_rows, "grad_out": grad_out, "master_value": master_value, "adam_first": adam_first, "adam_second": adam_second}


beta_first = 0.9
beta_second = 0.95
learning = 0.001
decay_rate = 0.1
epsilon = 1e-08

def attend_block(query_blk, grad_blk, key_win, value_win, allowed):
    ratio = HQ // HK
    scale = 1.0 / math.sqrt(DH)
    count = query_blk.shape[0]
    out_parts, dq_parts, dk_parts, dv_parts = ([], [], [], [])
    for group in range(HK):
        low = group * ratio * DH
        high = (group + 1) * ratio * DH
        query_group = query_blk[:, low:high].reshape(count, ratio, DH).astype(jnp.float32)
        grad_group = grad_blk[:, low:high].reshape(count, ratio, DH).astype(jnp.float32)
        key_group = key_win[:, group * DH:(group + 1) * DH].astype(jnp.float32)
        value_group = value_win[:, group * DH:(group + 1) * DH].astype(jnp.float32)
        scores = jnp.einsum('trd,sd->trs', query_group, key_group) * scale
        scores = jnp.where(allowed[:, None, :], scores, -jnp.inf)
        top = lax.optimization_barrier(jnp.max(scores, axis=2, keepdims=True))
        expd = jnp.exp(scores - top)
        probs = expd / lax.optimization_barrier(jnp.sum(expd, axis=2, keepdims=True))
        probs_low = probs.astype(jnp.bfloat16)
        out_group = jnp.einsum('trs,sd->trd', probs_low.astype(jnp.float32), value_group).astype(jnp.bfloat16)
        delta = lax.optimization_barrier(jnp.sum(grad_group * out_group.astype(jnp.float32), axis=2, keepdims=True))
        dprob = jnp.einsum('trd,sd->trs', grad_group, value_group)
        dscore = (probs * (dprob - delta)).astype(jnp.bfloat16).astype(jnp.float32)
        dq_group = (jnp.einsum('trs,sd->trd', dscore, key_group) * scale).astype(jnp.bfloat16)
        dk_group = jnp.einsum('trs,trd->sd', dscore, query_group) * scale
        dv_group = jnp.einsum('trs,trd->sd', probs_low.astype(jnp.float32), grad_group)
        out_parts.append(out_group.reshape(count, ratio * DH))
        dq_parts.append(dq_group.reshape(count, ratio * DH))
        dk_parts.append(dk_group)
        dv_parts.append(dv_group)
    return (jnp.concatenate(out_parts, 1), jnp.concatenate(dq_parts, 1), jnp.concatenate(dk_parts, 1), jnp.concatenate(dv_parts, 1))

def reference(hidden, queries, key_rows, grad_out, master_value, adam_first, adam_second):
    seq_len = hidden.shape[0]
    width = key_rows.shape[1]
    weight_low = master_value.astype(jnp.bfloat16)
    values = jnp.dot(hidden, weight_low, preferred_element_type=jnp.float32).astype(jnp.bfloat16)
    pad_keys = jnp.concatenate([jnp.zeros((WINDOW, width), jnp.bfloat16), key_rows], 0)
    pad_values = jnp.concatenate([jnp.zeros((WINDOW, width), jnp.bfloat16), values], 0)
    span_rows = WINDOW + TOK_DEV
    offsets = jnp.arange(span_rows, dtype=jnp.int32) - WINDOW
    relative = jnp.arange(TOK_DEV, dtype=jnp.int32)[:, None] - offsets[None, :]
    blocks = seq_len // TOK_DEV

    def advance(carry, block):
        key_acc, value_acc = carry
        start = (block * TOK_DEV).astype(jnp.int32)
        query_blk = lax.dynamic_slice_in_dim(queries, start, TOK_DEV, 0)
        grad_blk = lax.dynamic_slice_in_dim(grad_out, start, TOK_DEV, 0)
        key_win = lax.dynamic_slice_in_dim(pad_keys, start, span_rows, 0)
        value_win = lax.dynamic_slice_in_dim(pad_values, start, span_rows, 0)
        allowed = (relative >= 0) & (relative < WINDOW) & (start + offsets >= 0)[None, :]
        out_blk, dq_blk, dk_win, dv_win = attend_block(query_blk, grad_blk, key_win, value_win, allowed)
        key_acc = lax.dynamic_update_slice_in_dim(key_acc, lax.dynamic_slice_in_dim(key_acc, start, span_rows, 0) + dk_win, start, 0)
        value_acc = lax.dynamic_update_slice_in_dim(value_acc, lax.dynamic_slice_in_dim(value_acc, start, span_rows, 0) + dv_win, start, 0)
        return ((key_acc, value_acc), (out_blk, dq_blk))
    zeros_acc = jnp.zeros((seq_len + WINDOW, width), jnp.float32)
    (key_acc, value_acc), (out_all, dq_all) = lax.scan(advance, (zeros_acc, zeros_acc), jnp.arange(blocks, dtype=jnp.int32))
    attention = out_all.reshape(seq_len, queries.shape[1])
    grad_queries = dq_all.reshape(seq_len, queries.shape[1])
    grad_keys = key_acc[WINDOW:].astype(jnp.bfloat16)
    d_value = value_acc[WINDOW:].astype(jnp.bfloat16)
    grad_hidden = lax.dot_general(d_value, weight_low, (((1,), (1,)), ((), ())), preferred_element_type=jnp.float32).astype(jnp.bfloat16)
    grad_weight = lax.dot_general(hidden, d_value, (((0,), (0,)), ((), ())), preferred_element_type=jnp.float32)
    new_first = beta_first * adam_first + (1.0 - beta_first) * grad_weight
    new_second = beta_second * adam_second + (1.0 - beta_second) * grad_weight * grad_weight
    first_hat = new_first / (1.0 - beta_first ** OPT_STEP)
    second_hat = new_second / (1.0 - beta_second ** OPT_STEP)
    new_master = master_value - learning * (first_hat / (jnp.sqrt(second_hat) + epsilon) + decay_rate * master_value)
    return (attention, grad_queries, grad_keys, grad_hidden, new_master, new_first, new_second)
```

```python
import functools
import math

import jax
import jax.numpy as jnp
from jax import lax
from jax.experimental import pallas as pl
from jax.experimental.pallas import tpu as pltpu
from jax.sharding import PartitionSpec as P

HQ = 16
HK = 4
DH = 128
WINDOW = 512
OPT_STEP = 10
RATIO = HQ // HK
LANES = 128

beta_first = 0.9
beta_second = 0.95
learning = 0.001
decay_rate = 0.1
epsilon = 1e-08

BF = jnp.bfloat16
F32 = jnp.float32
MASKED = -1e30


def exchanged(block, mask):
    return lax.ppermute(block, "seq", [(i, i ^ mask) for i in range(lax.axis_size("seq"))])


def passed_along(block, distance):
    devices = range(lax.axis_size("seq"))
    return lax.ppermute(block, "seq", [(i, i + distance) for i in devices if i + distance in devices])


def in_core_order(core, own, other, axis):
    first = jnp.where(core == 0, own, other)
    second = jnp.where(core == 0, other, own)
    return jnp.concatenate([first, second], axis)


def chip_digits(chips):
    digits, shift = [], 0
    while (1 << shift) < chips:
        radix = min(4, chips >> shift)
        digits.append((shift, radix))
        shift += radix.bit_length() - 1
    return digits


def dotted(a, b, contract):
    return lax.dot_general(a, b, (contract, ((), ())), preferred_element_type=F32)


def stacked_heads(block):
    return jnp.concatenate([block[:, h * DH : (h + 1) * DH] for h in range(RATIO)], 0)


def forward_kernel(place, q_own, q_oth, g_own, g_oth, *refs, tok, reach):
    key_refs, (p_ref, *d_refs), acc = refs[: reach + 1], refs[reach + 1 : -1], refs[-1]
    core, chip = place[0], place[1]
    pair = 2 * tok
    span = WINDOW + tok
    keys = jnp.concatenate([ref[...] for ref in key_refs], 0)
    factor = math.log2(math.e) / math.sqrt(DH)
    row = lax.broadcasted_iota(jnp.int32, (tok, RATIO * tok), 0)
    query = lax.rem(lax.broadcasted_iota(jnp.int32, (tok, RATIO * tok), 1), tok)
    index = lax.broadcasted_iota(jnp.int32, (span, 1), 0)
    for b in range(2):
        q = stacked_heads(jnp.where(core == b, q_own[...], q_oth[...]))
        g = stacked_heads(jnp.where(core == b, g_own[...], g_oth[...]))
        s = dotted(keys[b * tok : b * tok + span], q, ((1,), (1,))) * factor
        s = s + jnp.where(index + b * tok + chip * pair >= WINDOW, 0.0, MASKED)
        s = jnp.concatenate(
            [
                jnp.where(row > query, s[:tok], MASKED),
                s[tok:WINDOW],
                jnp.where(row <= query, s[WINDOW:], MASKED),
            ],
            0,
        )
        top = jnp.max(s, axis=0, keepdims=True)
        e = jnp.exp2(s - top)
        p = (e * (1.0 / jnp.sum(e, axis=0, keepdims=True))).astype(BF)
        p_ref[0, b] = p
        d = dotted(p, g, ((1,), (0,)))
        if b == 0:
            acc[:span] = d
        else:
            acc[span:] = d[WINDOW:]
            acc[tok:span] += d[:WINDOW]
    for k, ref in enumerate(d_refs):
        low = (reach - k) * pair
        ref[...] = acc[low : low + pair].astype(ref.dtype)


def backward_kernel(place, q_own, q_oth, g_own, g_oth, *refs, tok, reach):
    key_refs, value_refs = refs[: reach + 1], refs[reach + 1 : 2 * reach + 2]
    p_ref, own_ref, send_ref, *d_refs = refs[2 * reach + 2 : -1]
    acc = refs[-1]
    core = place[0]
    pair = 2 * tok
    span = WINDOW + tok
    keys = jnp.concatenate([ref[...] for ref in key_refs], 0)
    values = jnp.concatenate([ref[...] for ref in value_refs], 0)
    scale = 1.0 / math.sqrt(DH)
    blocks = []
    for b in range(2):
        q = stacked_heads(jnp.where(core == b, q_own[...], q_oth[...]))
        g = stacked_heads(jnp.where(core == b, g_own[...], g_oth[...]))
        k_win = keys[b * tok : b * tok + span]
        v_win = values[b * tok : b * tok + span]
        p = p_ref[0, b]
        out = dotted(v_win, p, ((0,), (0,))).astype(BF)
        delta = jnp.sum(g.T.astype(F32) * out.astype(F32), axis=0, keepdims=True)
        dprob = dotted(v_win, g, ((1,), (1,)))
        dscore = (p.astype(F32) * (dprob - delta)).astype(BF)
        dk = dotted(dscore, q, ((1,), (0,))) * scale
        dq = (dotted(k_win, dscore, ((0,), (0,))) * scale).astype(BF)
        if b == 0:
            acc[:span] = dk
        else:
            acc[span:] = dk[WINDOW:]
            acc[tok:span] += dk[:WINDOW]
        halves = [
            jnp.concatenate([x[:, h * tok : (h + 1) * tok].T for h in range(RATIO)], 1)
            for x in (out, dq)
        ]
        blocks.append(halves)
    for i in range(2):
        own_ref[i] = jnp.where(core == 0, blocks[0][i], blocks[1][i])
        send_ref[i] = jnp.where(core == 0, blocks[1][i], blocks[0][i])
    for k, ref in enumerate(d_refs):
        low = (reach - k) * pair
        ref[...] = acc[low : low + pair].astype(ref.dtype)


def value_kernel(place, h_own, h_oth, *refs, digits, rows):
    pieces, (v_ref, w_ref) = refs[:-2], refs[-2:]
    core, chip = place[0], place[1]
    tok = h_own.shape[0]
    shift = digits[0][1].bit_length() - 1
    for k, piece in enumerate(pieces):
        for z in range(piece.shape[0]):
            target = lax.bitwise_xor(chip, k + (z << shift))
            w_ref[pl.ds(pl.multiple_of(target * rows, rows), rows), :] = piece[z]
    h = jnp.concatenate(
        [jnp.where(core == 0, h_own[...], h_oth[...]), jnp.where(core == 0, h_oth[...], h_own[...])],
        0,
    )
    v_ref[...] = dotted(h, w_ref[...], ((1,), (0,))).astype(BF)


def chip_values(place, hidden, hidden_other, pieces, digits, rows):
    tok, width = hidden.shape
    pair, columns = 2 * tok, pieces[0].shape[-1]
    if rows % 16:
        core, chip = place[0], place[1]
        blocks = jnp.stack(pieces, 1).reshape(-1, rows, columns)
        weight = blocks[jnp.arange(blocks.shape[0]) ^ chip].reshape(width, columns)
        h = in_core_order(core, hidden, hidden_other, 0)
        return dotted(h, weight, ((1,), (0,))).astype(BF), weight
    return pl.pallas_call(
        functools.partial(value_kernel, digits=digits, rows=rows),
        grid_spec=pltpu.PrefetchScalarGridSpec(
            num_scalar_prefetch=1,
            grid=(1,),
            in_specs=[pl.BlockSpec((tok, width), lambda g, s: (0, 0))] * 2
            + [pl.BlockSpec(piece.shape, lambda g, s: (0, 0, 0)) for piece in pieces],
            out_specs=[
                pl.BlockSpec((pair, columns), lambda g, s: (0, 0)),
                pl.BlockSpec((width, columns), lambda g, s: (0, 0)),
            ],
        ),
        out_shape=[
            jax.ShapeDtypeStruct((pair, columns), BF),
            jax.ShapeDtypeStruct((width, columns), BF),
        ],
        cost_estimate=pl.CostEstimate(
            flops=2 * pair * width * columns, bytes_accessed=3 << 20, transcendentals=0
        ),
        name="values",
    )(place, hidden, hidden_other, *pieces)


def shards(hidden, queries, key_rows, grad_out, master_value, adam_first, adam_second):
    tok, width = hidden.shape
    n = lax.axis_size("seq")
    chips = n // 2
    rows = master_value.shape[0]
    pair = 2 * tok
    reach = WINDOW // pair
    kv_half = key_rows.shape[1] // 2
    q_half = queries.shape[1] // 2
    groups = HK // 2
    wide = RATIO * DH
    span = WINDOW + tok
    digits = chip_digits(chips)
    index = lax.axis_index("seq")
    core, chip = index % 2, index // 2
    place = jnp.stack([core, chip]).astype(jnp.int32)

    def half(array, which, size):
        return lax.dynamic_slice_in_dim(array, which * size, size, 1)

    key_own = half(key_rows, core, kv_half)
    weight_low = master_value.astype(BF)
    near = exchanged(
        jnp.concatenate([half(key_rows, 1 - core, kv_half), half(weight_low, 1 - core, kv_half)], 0), 1
    )
    keys = [in_core_order(core, key_own, near[:tok], 0)]
    weight_block = in_core_order(core, half(weight_low, core, kv_half), near[tok:], 0)
    other = exchanged(
        jnp.concatenate([half(queries, 1 - core, q_half), half(grad_out, 1 - core, q_half)], 1), 1
    )
    hidden_other = exchanged(hidden, 1)
    for k in range(1, reach + 1):
        keys.append(passed_along(keys[0], 2 * k))

    pieces = [weight_block[None]]
    for shift, radix in digits[::-1]:
        block = jnp.stack(pieces, 1).reshape(-1, 2 * rows, kv_half)
        pieces = [block] + [exchanged(block, k << (shift + 1)) for k in range(1, radix)]

    def window_spec():
        return [pl.BlockSpec((pair, DH), lambda g, s: (0, g)) for _ in range(reach + 1)]

    half_specs = [
        pl.BlockSpec((tok, wide), lambda g, s: (0, groups * s[0] + g)),
        pl.BlockSpec((tok, wide), lambda g, s: (0, g)),
        pl.BlockSpec((tok, wide), lambda g, s: (0, groups * s[0] + g)),
        pl.BlockSpec((tok, wide), lambda g, s: (0, groups + g)),
    ]
    prob_spec = pl.BlockSpec((1, 2, span, RATIO * tok), lambda g, s: (g, 0, 0, 0))
    grad_shapes = [
        jax.ShapeDtypeStruct((pair, kv_half), BF if k else F32) for k in range(reach + 1)
    ]
    window_flops = 2 * groups * 2 * span * RATIO * tok * DH
    probs, *dv_parts = pl.pallas_call(
        functools.partial(forward_kernel, tok=tok, reach=reach),
        grid_spec=pltpu.PrefetchScalarGridSpec(
            num_scalar_prefetch=1,
            grid=(groups,),
            in_specs=half_specs + window_spec()[::-1],
            out_specs=[prob_spec] + window_spec(),
            scratch_shapes=[pltpu.VMEM(((reach + 1) * pair, DH), F32)],
        ),
        out_shape=[jax.ShapeDtypeStruct((groups, 2, span, RATIO * tok), BF)] + grad_shapes,
        cost_estimate=pl.CostEstimate(
            flops=2 * window_flops, bytes_accessed=8 << 20, transcendentals=window_flops // DH
        ),
        name="probs",
    )(place, queries, other, grad_out, other, *keys[::-1])
    dv_arrived = [passed_along(dv_parts[k], -2 * k) for k in range(1, reach + 1)]
    d_value = dv_parts[0]
    for term in dv_arrived:
        d_value = d_value + term
    d_value = d_value.astype(BF)

    hidden_pair = in_core_order(core, hidden, hidden_other, 0)
    total = dotted(hidden_pair, d_value, ((0,), (0,)))
    for shift, radix in digits:
        total = total.reshape(-1, radix, 2 * rows, kv_half)
        digit = (chip >> shift) % radix

        def portion(k):
            return lax.dynamic_index_in_dim(total, digit ^ k, 1, False)

        sent = [exchanged(portion(k).astype(BF), k << (shift + 1)) for k in range(1, radix)]
        kept = portion(0)
        for term in sent:
            kept = kept + term
        total = kept
    total = total.reshape(2, rows, kv_half)
    grad_weight = in_core_order(
        core,
        lax.dynamic_index_in_dim(total, core, 0, False),
        exchanged(lax.dynamic_index_in_dim(total, 1 - core, 0, False), 1),
        1,
    )

    values, weight_half = chip_values(place, hidden, hidden_other, pieces, digits, 2 * rows)
    value_win = [values] + [passed_along(values, 2 * k) for k in range(1, reach + 1)]

    out_specs = [pl.BlockSpec((2, tok, wide), lambda g, s: (0, 0, g))] * 2
    own, send, *dk_parts = pl.pallas_call(
        functools.partial(backward_kernel, tok=tok, reach=reach),
        grid_spec=pltpu.PrefetchScalarGridSpec(
            num_scalar_prefetch=1,
            grid=(groups,),
            in_specs=half_specs + window_spec() + window_spec() + [prob_spec],
            out_specs=out_specs + window_spec(),
            scratch_shapes=[pltpu.VMEM(((reach + 1) * pair, DH), F32)],
        ),
        out_shape=[jax.ShapeDtypeStruct((2, tok, q_half), BF)] * 2 + grad_shapes,
        cost_estimate=pl.CostEstimate(
            flops=4 * window_flops, bytes_accessed=8 << 20, transcendentals=0
        ),
        name="gradients",
    )(place, queries, other, grad_out, other, *keys[::-1], *value_win[::-1], probs)
    dk_arrived = [passed_along(dk_parts[k], -2 * k) for k in range(1, reach + 1)]
    dk = dk_parts[0]
    for term in dk_arrived:
        dk = dk + term
    dk = dk.astype(BF).reshape(2, tok, kv_half)
    arrived = exchanged(send, 1)
    attention = in_core_order(core, own[0], arrived[0], 1)
    grad_queries = in_core_order(core, own[1], arrived[1], 1)
    grad_keys = in_core_order(
        core,
        lax.dynamic_index_in_dim(dk, core, 0, False),
        exchanged(lax.dynamic_index_in_dim(dk, 1 - core, 0, False), 1),
        1,
    )

    d_value = d_value.reshape(2, tok, kv_half)
    hidden_sent = exchanged(
        dotted(lax.dynamic_index_in_dim(d_value, 1 - core, 0, False), weight_half, ((1,), (1,))).astype(BF),
        1,
    )
    grad_hidden = (
        dotted(lax.dynamic_index_in_dim(d_value, core, 0, False), weight_half, ((1,), (1,))) + hidden_sent
    ).astype(BF)

    new_first = beta_first * adam_first + (1.0 - beta_first) * grad_weight
    new_second = beta_second * adam_second + (1.0 - beta_second) * grad_weight * grad_weight
    first_hat = new_first / (1.0 - beta_first**OPT_STEP)
    second_hat = new_second / (1.0 - beta_second**OPT_STEP)
    new_master = master_value - learning * (
        first_hat / (jnp.sqrt(second_hat) + epsilon) + decay_rate * master_value
    )
    return (attention, grad_queries, grad_keys, grad_hidden, new_master, new_first, new_second)


def solution(mesh):
    return jax.shard_map(
        shards,
        mesh=mesh,
        in_specs=(P("seq", None),) * 7,
        out_specs=(P("seq", None),) * 7,
        check_vma=False,
    )
```

```python
import functools
import math

import jax
import jax.numpy as jnp
from jax import lax
from jax.experimental import pallas as pl
from jax.experimental.pallas import tpu as pltpu
from jax.sharding import PartitionSpec as P


HQ = 16
HK = 4
DH = 128
WINDOW = 512
OPT_STEP = 10
RATIO = HQ // HK

beta_first = 0.9
beta_second = 0.95
learning = 0.001
decay_rate = 0.1
epsilon = 1e-08

BF = jnp.bfloat16
F32 = jnp.float32
MASKED = -1e30


def exchanged(block, mask):
    return lax.ppermute(block, "seq", [(i, i ^ mask) for i in range(lax.axis_size("seq"))])


def passed_along(block, distance):
    n = lax.axis_size("seq")
    return lax.ppermute(block, "seq", [(i, (i + distance) % n) for i in range(n)])


def in_core_order(core, own, other, axis):
    first = jnp.where(core == 0, own, other)
    second = jnp.where(core == 0, other, own)
    return jnp.concatenate([first, second], axis)


def chip_digits(chips):
    digits, shift = [], 0
    while (1 << shift) < chips:
        radix = min(4, chips >> shift)
        digits.append((shift, radix))
        shift += radix.bit_length() - 1
    return digits


def dotted(a, b, contract):
    return lax.dot_general(a, b, (contract, ((), ())), preferred_element_type=F32)


def stacked_heads(block):
    return jnp.concatenate([block[:, h * DH : (h + 1) * DH] for h in range(RATIO)], 0)


def forward_kernel(place, q_own, q_oth, g_own, g_oth, *refs, tok, reach):
    key_refs, (p_ref, *d_refs), acc = refs[: reach + 1], refs[reach + 1 : -1], refs[-1]
    core, chip = place[0] & 1, place[0] >> 1
    pair = 2 * tok
    span = WINDOW + tok
    keys = jnp.concatenate([ref[...] for ref in key_refs], 0)
    factor = math.log2(math.e) / math.sqrt(DH)
    row = lax.broadcasted_iota(jnp.int32, (tok, RATIO * tok), 0)
    query = lax.rem(lax.broadcasted_iota(jnp.int32, (tok, RATIO * tok), 1), tok)
    index = lax.broadcasted_iota(jnp.int32, (span, 1), 0)
    for b in range(2):
        q = stacked_heads(jnp.where(core == b, q_own[...], q_oth[...]))
        g = stacked_heads(jnp.where(core == b, g_own[...], g_oth[...]))
        s = dotted(keys[b * tok : b * tok + span], q, ((1,), (1,))) * factor
        s = s + jnp.where(index + b * tok + chip * pair >= WINDOW, 0.0, MASKED)
        s = jnp.concatenate(
            [
                jnp.where(row > query, s[:tok], MASKED),
                s[tok:WINDOW],
                jnp.where(row <= query, s[WINDOW:], MASKED),
            ],
            0,
        )
        top = jnp.max(s, axis=0, keepdims=True)
        e = jnp.exp2(s - top)
        p = (e * (1.0 / jnp.sum(e, axis=0, keepdims=True))).astype(BF)
        p_ref[0, b] = p
        d = dotted(p, g, ((1,), (0,)))
        if b == 0:
            acc[:span] = d
        else:
            acc[span:] = d[WINDOW:]
            acc[tok:span] += d[:WINDOW]
    for k, ref in enumerate(d_refs):
        low = (reach - k) * pair
        ref[...] = acc[low : low + pair].astype(ref.dtype)


def backward_kernel(place, q_own, q_oth, g_own, g_oth, *refs, tok, reach):
    key_refs, value_refs = refs[: reach + 1], refs[reach + 1 : 2 * reach + 2]
    p_ref, own_ref, send_ref, *d_refs = refs[2 * reach + 2 : -1]
    acc = refs[-1]
    core = place[0] & 1
    pair = 2 * tok
    span = WINDOW + tok
    keys = jnp.concatenate([ref[...] for ref in key_refs], 0)
    values = jnp.concatenate([ref[...] for ref in value_refs], 0)
    scale = 1.0 / math.sqrt(DH)
    blocks = []
    for b in range(2):
        q = stacked_heads(jnp.where(core == b, q_own[...], q_oth[...]))
        g = stacked_heads(jnp.where(core == b, g_own[...], g_oth[...]))
        k_win = keys[b * tok : b * tok + span]
        v_win = values[b * tok : b * tok + span]
        p = p_ref[0, b]
        out = dotted(v_win, p, ((0,), (0,))).astype(BF)
        delta = jnp.sum(g.T.astype(F32) * out.astype(F32), axis=0, keepdims=True)
        dprob = dotted(v_win, g, ((1,), (1,)))
        dscore = (p.astype(F32) * (dprob - delta)).astype(BF)
        dk = dotted(dscore, q, ((1,), (0,))) * scale
        dq = (dotted(k_win, dscore, ((0,), (0,))) * scale).astype(BF)
        if b == 0:
            acc[:span] = dk
        else:
            acc[span:] = dk[WINDOW:]
            acc[tok:span] += dk[:WINDOW]
        halves = [
            jnp.concatenate([x[:, h * tok : (h + 1) * tok].T for h in range(RATIO)], 1)
            for x in (out, dq)
        ]
        blocks.append(halves)
    for i in range(2):
        own_ref[i] = jnp.where(core == 0, blocks[0][i], blocks[1][i])
        send_ref[i] = jnp.where(core == 0, blocks[1][i], blocks[0][i])
    for k, ref in enumerate(d_refs):
        low = (reach - k) * pair
        ref[...] = acc[low : low + pair].astype(ref.dtype)


def value_kernel(place, h_own, h_oth, *refs, digits, rows):
    pieces, (v_ref, w_ref) = refs[:-2], refs[-2:]
    core, chip = place[0] & 1, place[0] >> 1
    shift = digits[0][1].bit_length() - 1
    for k, piece in enumerate(pieces):
        for z in range(piece.shape[0]):
            target = lax.bitwise_xor(chip, k + (z << shift))
            w_ref[pl.ds(pl.multiple_of(target * rows, rows), rows), :] = piece[z]
    h = jnp.concatenate(
        [jnp.where(core == 0, h_own[...], h_oth[...]), jnp.where(core == 0, h_oth[...], h_own[...])],
        0,
    )
    v_ref[...] = dotted(h, w_ref[...], ((1,), (0,))).astype(BF)


def chip_values(place, hidden, hidden_other, pieces, digits, rows):
    tok, width = hidden.shape
    pair, columns = 2 * tok, pieces[0].shape[-1]
    if rows % 16:
        core, chip = place[0] & 1, place[0] >> 1
        blocks = jnp.stack(pieces, 1).reshape(-1, rows, columns)
        weight = blocks[jnp.arange(blocks.shape[0]) ^ chip].reshape(width, columns)
        h = in_core_order(core, hidden, hidden_other, 0)
        return dotted(h, weight, ((1,), (0,))).astype(BF), weight
    return pl.pallas_call(
        functools.partial(value_kernel, digits=digits, rows=rows),
        grid_spec=pltpu.PrefetchScalarGridSpec(
            num_scalar_prefetch=1,
            grid=(1,),
            in_specs=[pl.BlockSpec((tok, width), lambda g, s: (0, 0))] * 2
            + [pl.BlockSpec(piece.shape, lambda g, s: (0, 0, 0)) for piece in pieces],
            out_specs=[
                pl.BlockSpec((pair, columns), lambda g, s: (0, 0)),
                pl.BlockSpec((width, columns), lambda g, s: (0, 0)),
            ],
        ),
        out_shape=[
            jax.ShapeDtypeStruct((pair, columns), BF),
            jax.ShapeDtypeStruct((width, columns), BF),
        ],
        cost_estimate=pl.CostEstimate(
            flops=2 * pair * width * columns, bytes_accessed=3 << 20, transcendentals=0
        ),
        name="values",
    )(place, hidden, hidden_other, *pieces)


def step(hidden, queries, key_rows, grad_out, master_value, adam_first, adam_second):
    tok, _ = hidden.shape
    n = lax.axis_size("seq")
    chips = n // 2
    rows = master_value.shape[0]
    pair = 2 * tok
    reach = WINDOW // pair
    kv_half = key_rows.shape[1] // 2
    q_half = queries.shape[1] // 2
    groups = HK // 2
    wide = RATIO * DH
    span = WINDOW + tok
    digits = chip_digits(chips)
    index = lax.axis_index("seq")
    core, chip = index & 1, index >> 1
    place = index.astype(jnp.int32).reshape(1)

    def half(array, which, size):
        return lax.dynamic_slice_in_dim(array, which * size, size, 1)

    key_own = half(key_rows, core, kv_half)
    weight_low = master_value.astype(BF)
    near = exchanged(
        jnp.concatenate([half(key_rows, 1 - core, kv_half), half(weight_low, 1 - core, kv_half)], 0), 1
    )
    keys = [in_core_order(core, key_own, near[:tok], 0)]
    weight_block = in_core_order(core, half(weight_low, core, kv_half), near[tok:], 0)
    other = exchanged(
        jnp.concatenate([half(queries, 1 - core, q_half), half(grad_out, 1 - core, q_half)], 1), 1
    )
    hidden_other = exchanged(hidden, 1)
    for k in range(1, reach + 1):
        keys.append(passed_along(keys[0], 2 * k))

    pieces = [weight_block[None]]
    for shift, radix in digits[:0:-1]:
        block = jnp.stack(pieces, 1).reshape(-1, 2 * rows, kv_half)
        pieces = [block] + [exchanged(block, k << (shift + 1)) for k in range(1, radix)]

    block = jnp.stack(pieces, 1).reshape(-1, 2 * rows, kv_half)
    pieces = [block] + [exchanged(block, k << 1) for k in range(1, digits[0][1])]

    def window_spec():
        return [pl.BlockSpec((pair, DH), lambda g, s: (0, g)) for _ in range(reach + 1)]

    half_specs = [
        pl.BlockSpec((tok, wide), lambda g, s: (0, groups * (s[0] & 1) + g)),
        pl.BlockSpec((tok, wide), lambda g, s: (0, g)),
        pl.BlockSpec((tok, wide), lambda g, s: (0, groups * (s[0] & 1) + g)),
        pl.BlockSpec((tok, wide), lambda g, s: (0, groups + g)),
    ]
    prob_spec = pl.BlockSpec((1, 2, span, RATIO * tok), lambda g, s: (g, 0, 0, 0))
    grad_shapes = [
        jax.ShapeDtypeStruct((pair, kv_half), BF if k else F32) for k in range(reach + 1)
    ]
    window_flops = 2 * groups * 2 * span * RATIO * tok * DH
    probs, *dv_parts = pl.pallas_call(
        functools.partial(forward_kernel, tok=tok, reach=reach),
        grid_spec=pltpu.PrefetchScalarGridSpec(
            num_scalar_prefetch=1,
            grid=(groups,),
            in_specs=half_specs + window_spec()[::-1],
            out_specs=[prob_spec] + window_spec(),
            scratch_shapes=[pltpu.VMEM(((reach + 1) * pair, DH), F32)],
        ),
        out_shape=[jax.ShapeDtypeStruct((groups, 2, span, RATIO * tok), BF)] + grad_shapes,
        cost_estimate=pl.CostEstimate(
            flops=2 * window_flops, bytes_accessed=8 << 20, transcendentals=window_flops // DH
        ),
        name="probs",
    )(place, queries, other, grad_out, other, *keys[::-1])
    dv_arrived = [passed_along(dv_parts[k], -2 * k) for k in range(1, reach + 1)]
    d_value = dv_parts[0]
    for term in dv_arrived:
        d_value = d_value + term
    d_value = d_value.astype(BF)

    hidden_pair = in_core_order(core, hidden, hidden_other, 0)
    total = dotted(hidden_pair, d_value, ((0,), (0,)))
    total, *pieces = lax.optimization_barrier((total, *pieces))

    def staged(total, stage):
        shift, radix = digits[stage]
        total = total.reshape(-1, radix, 2 * rows, kv_half)
        digit = (chip >> shift) & (radix - 1)

        def portion(k):
            return lax.dynamic_index_in_dim(total, digit ^ k, 1, False)

        sent = [exchanged(portion(k).astype(BF), k << (shift + 1)) for k in range(1, radix)]
        return portion(0), sent

    values, weight_half = chip_values(place, hidden, hidden_other, pieces, digits, 2 * rows)
    value_win = [values] + [passed_along(values, 2 * k) for k in range(1, reach + 1)]

    out_specs = [pl.BlockSpec((2, tok, wide), lambda g, s: (0, 0, g))] * 2
    own, send, *dk_parts = pl.pallas_call(
        functools.partial(backward_kernel, tok=tok, reach=reach),
        grid_spec=pltpu.PrefetchScalarGridSpec(
            num_scalar_prefetch=1,
            grid=(groups,),
            in_specs=half_specs + window_spec() + window_spec() + [prob_spec],
            out_specs=out_specs + window_spec(),
            scratch_shapes=[pltpu.VMEM(((reach + 1) * pair, DH), F32)],
        ),
        out_shape=[jax.ShapeDtypeStruct((2, tok, q_half), BF)] * 2 + grad_shapes,
        cost_estimate=pl.CostEstimate(
            flops=4 * window_flops, bytes_accessed=8 << 20, transcendentals=0
        ),
        name="gradients",
    )(place, queries, other, grad_out, other, *keys[::-1], *value_win[::-1], probs)
    dk_arrived = [passed_along(dk_parts[k], -2 * k) for k in range(1, reach + 1)]
    arrived = exchanged(send, 1)
    for stage in range(len(digits) - 1):
        total, terms = staged(total, stage)
        for term in terms:
            total = total + term
    kept, terms = staged(total, len(digits) - 1)
    attention = in_core_order(core, own[0], arrived[0], 1)
    grad_queries = in_core_order(core, own[1], arrived[1], 1)

    d_value = d_value.reshape(2, tok, kv_half)
    part, part_send = [
        dotted(lax.dynamic_index_in_dim(d_value, which, 0, False), weight_half, ((1,), (1,)))
        for which in (core, 1 - core)
    ]
    part_arrived = exchanged(part_send.astype(BF), 1)
    part, part_arrived = lax.optimization_barrier((part, part_arrived))
    grad_hidden = (part + part_arrived).astype(BF)

    kept, dk, attention, grad_queries, grad_hidden, *terms = lax.optimization_barrier(
        (kept, dk_parts[0], attention, grad_queries, grad_hidden, *terms)
    )
    for term in dk_arrived:
        dk = dk + term
    dk = dk.astype(BF).reshape(2, tok, kv_half)
    grad_keys = in_core_order(
        core,
        lax.dynamic_index_in_dim(dk, core, 0, False),
        exchanged(lax.dynamic_index_in_dim(dk, 1 - core, 0, False), 1),
        1,
    )
    for term in terms:
        kept = kept + term
    total = kept.reshape(2, rows, kv_half)
    grad_weight = in_core_order(
        core,
        lax.dynamic_index_in_dim(total, core, 0, False),
        exchanged(lax.dynamic_index_in_dim(total, 1 - core, 0, False), 1),
        1,
    )

    new_first = beta_first * adam_first + (1.0 - beta_first) * grad_weight
    new_second = beta_second * adam_second + (1.0 - beta_second) * grad_weight * grad_weight
    first_hat = new_first / (1.0 - beta_first**OPT_STEP)
    second_hat = new_second / (1.0 - beta_second**OPT_STEP)
    new_master = master_value - learning * (
        first_hat / (jnp.sqrt(second_hat) + epsilon) + decay_rate * master_value
    )
    return (attention, grad_queries, grad_keys, grad_hidden, new_master, new_first, new_second)


def solution(mesh):
    return jax.shard_map(
        step,
        mesh=mesh,
        in_specs=(P("seq", None),) * 7,
        out_specs=(P("seq", None),) * 7,
        check_vma=False,
    )
```

```python
import functools
import math

import jax
import jax.numpy as jnp
from jax import lax
from jax.experimental import pallas as pl
from jax.experimental.pallas import tpu as pltpu
from jax.sharding import PartitionSpec as P


HQ = 16
HK = 4
DH = 128
WINDOW = 512
OPT_STEP = 10
RATIO = HQ // HK

beta_first = 0.9
beta_second = 0.95
learning = 0.001
decay_rate = 0.1
epsilon = 1e-08

BF = jnp.bfloat16
F32 = jnp.float32
MASKED = -1e30


def exchanged(block, mask):
    return lax.ppermute(block, "seq", [(i, i ^ mask) for i in range(lax.axis_size("seq"))])


def passed_along(block, distance):
    n = lax.axis_size("seq")
    return lax.ppermute(block, "seq", [(i, (i + distance) % n) for i in range(n)])


def in_core_order(core, own, other, axis):
    first = jnp.where(core == 0, own, other)
    second = jnp.where(core == 0, other, own)
    return jnp.concatenate([first, second], axis)


def chip_digits(chips):
    digits, shift = [], 0
    while (1 << shift) < chips:
        radix = min(4, chips >> shift)
        digits.append((shift, radix))
        shift += radix.bit_length() - 1
    return digits


def dotted(a, b, contract):
    return lax.dot_general(a, b, (contract, ((), ())), preferred_element_type=F32)


def stacked_heads(block):
    return jnp.concatenate([block[:, h * DH : (h + 1) * DH] for h in range(RATIO)], 0)


def forward_kernel(place, q_own, q_oth, g_own, g_oth, *refs, tok, reach):
    key_refs, (p_ref, *d_refs), acc = refs[: reach + 1], refs[reach + 1 : -1], refs[-1]
    core, chip = place[0] & 1, place[0] >> 1
    pair = 2 * tok
    span = WINDOW + tok
    keys = jnp.concatenate([ref[...] for ref in key_refs], 0)
    factor = math.log2(math.e) / math.sqrt(DH)
    row = lax.broadcasted_iota(jnp.int32, (tok, RATIO * tok), 0)
    query = lax.rem(lax.broadcasted_iota(jnp.int32, (tok, RATIO * tok), 1), tok)
    index = lax.broadcasted_iota(jnp.int32, (span, 1), 0)
    for b in range(2):
        q = stacked_heads(jnp.where(core == b, q_own[...], q_oth[...]))
        g = stacked_heads(jnp.where(core == b, g_own[...], g_oth[...]))
        s = dotted(keys[b * tok : b * tok + span], q, ((1,), (1,))) * factor
        s = s + jnp.where(index + b * tok + chip * pair >= WINDOW, 0.0, MASKED)
        s = jnp.concatenate(
            [
                jnp.where(row > query, s[:tok], MASKED),
                s[tok:WINDOW],
                jnp.where(row <= query, s[WINDOW:], MASKED),
            ],
            0,
        )
        top = jnp.max(s, axis=0, keepdims=True)
        e = jnp.exp2(s - top)
        p = (e * (1.0 / jnp.sum(e, axis=0, keepdims=True))).astype(BF)
        p_ref[0, b] = p
        d = dotted(p, g, ((1,), (0,)))
        if b == 0:
            acc[:span] = d
        else:
            acc[span:] = d[WINDOW:]
            acc[tok:span] += d[:WINDOW]
    for k, ref in enumerate(d_refs):
        low = (reach - k) * pair
        ref[...] = acc[low : low + pair].astype(ref.dtype)


def backward_kernel(place, q_own, q_oth, g_own, g_oth, *refs, tok, reach):
    key_refs, value_refs = refs[: reach + 1], refs[reach + 1 : 2 * reach + 2]
    p_ref, own_ref, send_ref, *d_refs = refs[2 * reach + 2 : -1]
    acc = refs[-1]
    core = place[0] & 1
    pair = 2 * tok
    span = WINDOW + tok
    keys = jnp.concatenate([ref[...] for ref in key_refs], 0)
    values = jnp.concatenate([ref[...] for ref in value_refs], 0)
    scale = 1.0 / math.sqrt(DH)
    blocks = []
    for b in range(2):
        q = stacked_heads(jnp.where(core == b, q_own[...], q_oth[...]))
        g = stacked_heads(jnp.where(core == b, g_own[...], g_oth[...]))
        k_win = keys[b * tok : b * tok + span]
        v_win = values[b * tok : b * tok + span]
        p = p_ref[0, b]
        out = dotted(v_win, p, ((0,), (0,))).astype(BF)
        delta = jnp.sum(g.T.astype(F32) * out.astype(F32), axis=0, keepdims=True)
        dprob = dotted(v_win, g, ((1,), (1,)))
        dscore = (p.astype(F32) * (dprob - delta)).astype(BF)
        dk = dotted(dscore, q, ((1,), (0,))) * scale
        dq = (dotted(k_win, dscore, ((0,), (0,))) * scale).astype(BF)
        if b == 0:
            acc[:span] = dk
        else:
            acc[span:] = dk[WINDOW:]
            acc[tok:span] += dk[:WINDOW]
        halves = [
            jnp.concatenate([x[:, h * tok : (h + 1) * tok].T for h in range(RATIO)], 1)
            for x in (out, dq)
        ]
        blocks.append(halves)
    for i in range(2):
        own_ref[i] = jnp.where(core == 0, blocks[0][i], blocks[1][i])
        send_ref[i] = jnp.where(core == 0, blocks[1][i], blocks[0][i])
    for k, ref in enumerate(d_refs):
        low = (reach - k) * pair
        ref[...] = acc[low : low + pair].astype(ref.dtype)


def value_kernel(place, h_own, h_oth, *refs, digits, rows):
    pieces, (v_ref, w_ref) = refs[:-2], refs[-2:]
    core, chip = place[0] & 1, place[0] >> 1
    shift = digits[0][1].bit_length() - 1
    for k, piece in enumerate(pieces):
        for z in range(piece.shape[0]):
            target = lax.bitwise_xor(chip, k + (z << shift))
            w_ref[pl.ds(pl.multiple_of(target * rows, rows), rows), :] = piece[z]
    h = jnp.concatenate(
        [jnp.where(core == 0, h_own[...], h_oth[...]), jnp.where(core == 0, h_oth[...], h_own[...])],
        0,
    )
    v_ref[...] = dotted(h, w_ref[...], ((1,), (0,))).astype(BF)


def chip_values(place, hidden, hidden_other, pieces, digits, rows):
    tok, width = hidden.shape
    pair, columns = 2 * tok, pieces[0].shape[-1]
    if rows % 16:
        core, chip = place[0] & 1, place[0] >> 1
        blocks = jnp.stack(pieces, 1).reshape(-1, rows, columns)
        weight = blocks[jnp.arange(blocks.shape[0]) ^ chip].reshape(width, columns)
        h = in_core_order(core, hidden, hidden_other, 0)
        return dotted(h, weight, ((1,), (0,))).astype(BF), weight
    return pl.pallas_call(
        functools.partial(value_kernel, digits=digits, rows=rows),
        grid_spec=pltpu.PrefetchScalarGridSpec(
            num_scalar_prefetch=1,
            grid=(1,),
            in_specs=[pl.BlockSpec((tok, width), lambda g, s: (0, 0))] * 2
            + [pl.BlockSpec(piece.shape, lambda g, s: (0, 0, 0)) for piece in pieces],
            out_specs=[
                pl.BlockSpec((pair, columns), lambda g, s: (0, 0)),
                pl.BlockSpec((width, columns), lambda g, s: (0, 0)),
            ],
        ),
        out_shape=[
            jax.ShapeDtypeStruct((pair, columns), BF),
            jax.ShapeDtypeStruct((width, columns), BF),
        ],
        cost_estimate=pl.CostEstimate(
            flops=2 * pair * width * columns, bytes_accessed=3 << 20, transcendentals=0
        ),
        name="values",
    )(place, hidden, hidden_other, *pieces)


def first_kernel(place, key_ref, weight_ref, out_ref):
    core = place[0] & 1
    tok, half = key_ref.shape[0], key_ref.shape[1] // 2
    out_ref[:tok] = jnp.where(core == 0, key_ref[:, half:], key_ref[:, :half])
    out_ref[tok:] = jnp.where(core == 0, weight_ref[:, half:], weight_ref[:, :half]).astype(BF)


def step(hidden, queries, key_rows, grad_out, master_value, adam_first, adam_second):
    tok, _ = hidden.shape
    n = lax.axis_size("seq")
    chips = n // 2
    rows = master_value.shape[0]
    pair = 2 * tok
    reach = WINDOW // pair
    kv_half = key_rows.shape[1] // 2
    q_half = queries.shape[1] // 2
    groups = HK // 2
    wide = RATIO * DH
    span = WINDOW + tok
    digits = chip_digits(chips)
    index = lax.axis_index("seq")
    core, chip = index & 1, index >> 1
    place = index.astype(jnp.int32).reshape(1)

    def half(array, which, size):
        return lax.dynamic_slice_in_dim(array, which * size, size, 1)

    key_own = half(key_rows, core, kv_half)
    weight_low = master_value.astype(BF)
    near = exchanged(
        pl.pallas_call(
            first_kernel,
            grid_spec=pltpu.PrefetchScalarGridSpec(
                num_scalar_prefetch=1,
                grid=(1,),
                in_specs=[
                    pl.BlockSpec(array.shape, lambda g, s: (0, 0)) for array in (key_rows, master_value)
                ],
                out_specs=pl.BlockSpec((tok + rows, kv_half), lambda g, s: (0, 0)),
            ),
            out_shape=jax.ShapeDtypeStruct((tok + rows, kv_half), BF),
            cost_estimate=pl.CostEstimate(flops=0, bytes_accessed=1 << 18, transcendentals=0),
            name="first",
        )(place, key_rows, master_value),
        1,
    )
    keys = [in_core_order(core, key_own, near[:tok], 0)]
    weight_block = in_core_order(core, half(weight_low, core, kv_half), near[tok:], 0)
    other = exchanged(
        jnp.concatenate([half(queries, 1 - core, q_half), half(grad_out, 1 - core, q_half)], 1), 1
    )
    hidden_other = exchanged(hidden, 1)
    for k in range(1, reach + 1):
        keys.append(passed_along(keys[0], 2 * k))

    pieces = [weight_block[None]]
    for shift, radix in digits[:0:-1]:
        block = jnp.stack(pieces, 1).reshape(-1, 2 * rows, kv_half)
        pieces = [block] + [exchanged(block, k << (shift + 1)) for k in range(1, radix)]

    block = jnp.stack(pieces, 1).reshape(-1, 2 * rows, kv_half)
    pieces = [block] + [exchanged(block, k << 1) for k in range(1, digits[0][1])]

    def window_spec():
        return [pl.BlockSpec((pair, DH), lambda g, s: (0, g)) for _ in range(reach + 1)]

    half_specs = [
        pl.BlockSpec((tok, wide), lambda g, s: (0, groups * (s[0] & 1) + g)),
        pl.BlockSpec((tok, wide), lambda g, s: (0, g)),
        pl.BlockSpec((tok, wide), lambda g, s: (0, groups * (s[0] & 1) + g)),
        pl.BlockSpec((tok, wide), lambda g, s: (0, groups + g)),
    ]
    prob_spec = pl.BlockSpec((1, 2, span, RATIO * tok), lambda g, s: (g, 0, 0, 0))
    grad_shapes = [
        jax.ShapeDtypeStruct((pair, kv_half), BF if k else F32) for k in range(reach + 1)
    ]
    window_flops = 2 * groups * 2 * span * RATIO * tok * DH
    probs, *dv_parts = pl.pallas_call(
        functools.partial(forward_kernel, tok=tok, reach=reach),
        grid_spec=pltpu.PrefetchScalarGridSpec(
            num_scalar_prefetch=1,
            grid=(groups,),
            in_specs=half_specs + window_spec(),
            out_specs=[prob_spec] + window_spec(),
            scratch_shapes=[pltpu.VMEM(((reach + 1) * pair, DH), F32)],
        ),
        out_shape=[jax.ShapeDtypeStruct((groups, 2, span, RATIO * tok), BF)] + grad_shapes,
        cost_estimate=pl.CostEstimate(
            flops=2 * window_flops, bytes_accessed=8 << 20, transcendentals=window_flops // DH
        ),
        name="probs",
    )(place, queries, other, grad_out, other, *keys[::-1])
    dv_arrived = [passed_along(dv_parts[k], -2 * k) for k in range(1, reach + 1)]
    d_value = dv_parts[0]
    for term in dv_arrived:
        d_value = d_value + term
    d_value = d_value.astype(BF)

    hidden_pair = in_core_order(core, hidden, hidden_other, 0)
    total = dotted(hidden_pair, d_value, ((0,), (0,))).astype(BF)

    def staged(total, stage):
        shift, radix = digits[stage]
        total = total.reshape(-1, radix, 2 * rows, kv_half)
        digit = (chip >> shift) & (radix - 1)

        def portion(k):
            return lax.dynamic_index_in_dim(total, digit ^ k, 1, False)

        sent = [exchanged(portion(k).astype(BF), k << (shift + 1)) for k in range(1, radix)]
        return portion(0).astype(F32), sent

    values, weight_half = chip_values(place, hidden, hidden_other, pieces, digits, 2 * rows)
    value_win = [values] + [passed_along(values, 2 * k) for k in range(1, reach + 1)]

    out_specs = [pl.BlockSpec((2, tok, wide), lambda g, s: (0, 0, g))] * 2
    own, send, *dk_parts = pl.pallas_call(
        functools.partial(backward_kernel, tok=tok, reach=reach),
        grid_spec=pltpu.PrefetchScalarGridSpec(
            num_scalar_prefetch=1,
            grid=(groups,),
            in_specs=half_specs + window_spec() + window_spec() + [prob_spec],
            out_specs=out_specs + window_spec(),
            scratch_shapes=[pltpu.VMEM(((reach + 1) * pair, DH), F32)],
        ),
        out_shape=[jax.ShapeDtypeStruct((2, tok, q_half), BF)] * 2 + grad_shapes,
        cost_estimate=pl.CostEstimate(
            flops=4 * window_flops, bytes_accessed=8 << 20, transcendentals=0
        ),
        name="gradients",
    )(place, queries, other, grad_out, other, *keys[::-1], *value_win[::-1], probs)
    dk_arrived = [passed_along(dk_parts[k], -2 * k) for k in range(1, reach + 1)]
    arrived = exchanged(send, 1)
    for stage in range(len(digits) - 1):
        total, terms = staged(total, stage)
        for term in terms:
            total = total + term
    kept, terms = staged(total, len(digits) - 1)
    attention = in_core_order(core, own[0], arrived[0], 1)
    grad_queries = in_core_order(core, own[1], arrived[1], 1)

    d_halves = d_value.reshape(2, tok, kv_half)
    part, part_send = [
        dotted(lax.dynamic_index_in_dim(d_halves, which, 0, False), weight_half, ((1,), (1,))).astype(BF)
        for which in (core, 1 - core)
    ]
    part_arrived = exchanged(part_send, 1)
    grad_hidden = (part.astype(F32) + part_arrived.astype(F32)).astype(BF)

    kept, dk, attention, grad_queries, grad_hidden, *terms = lax.optimization_barrier(
        (kept, dk_parts[0], attention, grad_queries, grad_hidden, *terms)
    )
    for term in dk_arrived:
        dk = dk + term
    dk = dk.astype(BF).reshape(2, tok, kv_half)
    grad_keys = in_core_order(
        core,
        lax.dynamic_index_in_dim(dk, core, 0, False),
        exchanged(lax.dynamic_index_in_dim(dk, 1 - core, 0, False), 1),
        1,
    )
    for term in terms:
        kept = kept + term
    total = kept.reshape(2, rows, kv_half)
    grad_weight = in_core_order(
        core,
        lax.dynamic_index_in_dim(total, core, 0, False),
        exchanged(lax.dynamic_index_in_dim(total, 1 - core, 0, False), 1),
        1,
    )

    new_first = beta_first * adam_first + (1.0 - beta_first) * grad_weight
    new_second = beta_second * adam_second + (1.0 - beta_second) * grad_weight * grad_weight
    first_hat = new_first / (1.0 - beta_first**OPT_STEP)
    second_hat = new_second / (1.0 - beta_second**OPT_STEP)
    new_master = master_value - learning * (
        first_hat / (jnp.sqrt(second_hat) + epsilon) + decay_rate * master_value
    )
    return (attention, grad_queries, grad_keys, grad_hidden, new_master, new_first, new_second)


def solution(mesh):
    return jax.shard_map(
        step,
        mesh=mesh,
        in_specs=(P("seq", None),) * 7,
        out_specs=(P("seq", None),) * 7,
        check_vma=False,
    )
```
